32 devices in a mesh: dp: 16 (over z, x, core), mp: 2 (over y).
Axes of the slice: x: 2, y: 2, z: 4, core: 2. Of those that a mesh axis runs over, the one named last changes fastest.
Arguments:
- activations: bfloat16 [256, 9216], P('mp', 'dp'), may hold values from -6 to 6
- block_values: bfloat16 [384, 20, 128, 128], P('dp'), may hold values from -0.125 to 0.125
- block_rows: int32 [384, 20], P('dp'), may hold values from 0 to 71, all different within a row
- cotangent: bfloat16 [256, 49152], P('mp', 'dp'), may hold values from -6 to 6
Outputs:
- gelu_out: bfloat16 [256, 49152], P('mp', 'dp')
- input_grad: bfloat16 [256, 9216], P('mp', 'dp')
- block_grad: float32 [384, 20, 128, 128], P('dp', 'mp')
The draws below stay inside these ranges and needn't reach their ends.
Inputs may be any that keep to these rules, and one draw needn't show every extreme that they name: `block_rows`: the 20 entries of each column block are different block rows; every block row is named somewhere.
All inputs are finite; a program needn't handle non-finite values.
Results may differ from the reference program's by a relative error of at most 0.0049.
Values may be sent and summed in bfloat16 or wider, within the bound.
No kernel may reach another device: no remote copies, remote signals or barrier semaphores. Data moves between devices by JAX's collectives and lax.ppermute only.
A program may use at most 128 MiB of HBM per device.

```python
import jax
import jax.numpy as jnp
from jax import lax

D = 9216
FF = 49152
BLK = 128
KB = 20
TOKENS = 256
RB = 72
NCB = 384


def level_of(rng, dims, cuts, low, top_value):
    loudness = 1.0
    for dim, blocks in cuts:
        heights = jax.random.uniform(jax.random.fold_in(jax.random.fold_in(rng, 6), dim), (blocks,), jnp.float32, low / len(cuts), top_value / len(cuts))
        loudness = loudness * jnp.repeat(jnp.exp(heights), dims[dim] // blocks).reshape((-1,) + (1,) * (len(dims) - 1 - dim))
    return loudness


def distinct(key, rows, amount, top, lift):
    sequence = jax.random.permutation(jax.random.fold_in(key, 1), amount)
    pull = sequence
    for power in range(3):
        pull = pull * pull // amount
    pull = pull * lift // amount
    lots = jax.random.randint(jax.random.fold_in(key, 2), (rows, amount), 0, 4096) + pull
    holders = jax.random.permutation(jax.random.fold_in(key, 3), rows)[jnp.arange(amount) % rows]
    lots = jnp.where(jnp.arange(rows)[:, None] == holders[None, :], 1 << 14, lots)
    merit = lots * amount + jnp.arange(amount)
    return lax.top_k(merit.astype(jnp.int32), top)[1].astype(jnp.int32)


def scatter_about(stream_key, shape, width, bound, cuts=(), dtype=jnp.bfloat16):
    result = width * jax.random.normal(stream_key, shape, jnp.float32)
    if cuts:
        result = result * level_of(stream_key, shape, cuts, -0.22, 0.18)
    return jnp.clip(result, -bound, bound).astype(dtype)


def setup_inputs(seed: int = 0) -> dict:
    seeds = jax.random.split(jax.random.key(seed), 5)
    return {
        "activations": scatter_about(seeds[0], (TOKENS, D), 1.0, 6.0, ((0, 2), (1, 16))),
        "block_values": scatter_about(seeds[1], (NCB, KB, BLK, BLK), (KB * BLK) ** -0.5, 0.125, ((0, 16),)),
        "block_rows": distinct(seeds[2], NCB, RB, KB, 2275),
        "cotangent": scatter_about(seeds[3], (TOKENS, FF), 1.0, 6.0, ((0, 2), (1, 16))),
    }


def gelu_tanh(values):
    return jax.nn.gelu(values, approximate=True)

def reference(activations, block_values, block_rows, cotangent):
    num_tokens = activations.shape[0]
    x_blocks = activations.reshape(num_tokens, RB, BLK)
    cot_columns = jnp.transpose(cotangent.reshape(num_tokens, NCB, BLK), (1, 0, 2))

    def column(running, column_data):
        w_column, row_list, cot_column = column_data
        picked_rows = jnp.take(x_blocks, row_list, axis=1).astype(jnp.float32)
        weights32 = w_column.astype(jnp.float32)
        pre_act = jnp.einsum('tki,kij->tj', picked_rows, weights32, precision=lax.Precision.HIGHEST)
        activated = gelu_tanh(pre_act).astype(jnp.bfloat16)
        unused, pull_back = jax.vjp(gelu_tanh, pre_act)
        slopes = pull_back(cot_column.astype(jnp.float32))[0].astype(jnp.bfloat16)
        slopes32 = slopes.astype(jnp.float32)
        contrib = jnp.einsum('tj,kij->tki', slopes32, weights32, precision=lax.Precision.HIGHEST)
        running = running.at[:, row_list].add(contrib)
        grads = jnp.einsum('tki,tj->kij', picked_rows, slopes32, precision=lax.Precision.HIGHEST)
        return (running, (activated, grads))
    start_grad = jnp.zeros((num_tokens, RB, BLK), jnp.float32)
    total_grad, (activated, block_grad) = lax.scan(column, start_grad, (block_values, block_rows, cot_columns))
    gelu_out = jnp.transpose(activated, (1, 0, 2)).reshape(num_tokens, FF)
    input_grad = total_grad.reshape(num_tokens, D).astype(jnp.bfloat16)
    return (gelu_out, input_grad, block_grad)
```

```python
import functools

import jax
import jax.numpy as jnp
import numpy as np
from jax import lax
from jax.experimental import pallas as pl
from jax.experimental.pallas import tpu as pltpu
from jax.sharding import PartitionSpec as P

CORES = 2
SIDES = 2
MAX_LINE = 8


SQRT_2_PI = float(np.sqrt(2.0 / np.pi))
CUBIC = 0.044715


def forward_kernel(n_in, groups, sets, rows_s, offs_s, *refs):
    x_refs, refs = refs[:n_in], refs[n_in:]
    w_ref, cot_ref, gelu_ref, slope_ref = refs[:4]
    dx_refs, refs = refs[4 : 4 + len(groups)], refs[4 + len(groups) :]
    xt, xs, acc, w, cot, gelu, slopes, x_sem, w_sem, cot_sem, out_sem, dx_sem = refs
    cols, slots, side, _ = w.shape
    blocks = xs.shape[0]

    def shard(j):
        rows = x_refs[j].shape[0]
        target = xt.at[pl.ds(pl.multiple_of(offs_s[j], 16), rows), :]
        return pltpu.make_async_copy(x_refs[j], target, x_sem.at[j])

    def weights(c):
        return pltpu.make_async_copy(w_ref.at[c], w.at[c], w_sem.at[c])

    def outs(c):
        return (
            pltpu.make_async_copy(gelu.at[c], gelu_ref.at[:, column(c)], out_sem.at[0, c]),
            pltpu.make_async_copy(slopes.at[c], slope_ref.at[:, column(c)], out_sem.at[1, c]),
        )

    def column(c):
        return pl.ds(pl.multiple_of(c * side, side), side)

    def block(r):
        return pl.ds(pl.multiple_of(r * side, side), side)

    for j in range(n_in):
        shard(j).start()
    cotangent = pltpu.make_async_copy(cot_ref, cot, cot_sem)
    cotangent.start()

    def load(c, carry):
        weights(c).start()
        return carry

    def clear(r, carry):
        acc[r] = jnp.zeros(acc.shape[1:], acc.dtype)
        return carry

    lax.fori_loop(0, blocks, clear, 0)
    for j in range(n_in):
        shard(j).wait()
    lax.fori_loop(0, cols, load, 0)

    def turn(r, carry):
        xs[r] = xt[block(r), :].T
        return carry

    lax.fori_loop(0, blocks, turn, 0, unroll=4)
    cotangent.wait()

    def ahead(c):
        row = [rows_s[c, k] for k in range(slots)]
        v = 0.0
        for k in range(0, slots, 2):
            v = v + jnp.dot(
                jnp.concatenate([xs[r] for r in row[k : k + 2]], axis=1),
                w[c, k : k + 2].reshape(2 * side, side),
                preferred_element_type=jnp.float32,
            )
        v2 = v * v
        t = jnp.tanh(SQRT_2_PI * (v + CUBIC * (v * v2)))
        half = 0.5 * (1.0 + t)
        gelu[c] = (v * half).astype(gelu.dtype)
        slope = half + (0.5 * v) * (1.0 - t * t) * (SQRT_2_PI * (1.0 + (3.0 * CUBIC) * v2))
        slopes[c] = (cot[:, column(c)].astype(jnp.float32) * slope).astype(slopes.dtype)

    def back(c):
        turned = slopes[c].T
        step = 2 if slots % 2 == 0 else 1
        for k in range(0, slots, step):
            part = jnp.dot(
                w[c, k : k + step].reshape(step * side, side),
                turned,
                preferred_element_type=jnp.float32,
            )
            for i in range(step):
                acc[rows_s[c, k + i]] += part[i * side : (i + 1) * side, :]

    def send(c):
        for copy in outs(c):
            copy.start()

    def one(c, carry):
        weights(c + 1).wait()
        send(c)
        ahead(c + 1)
        back(c)
        return carry

    weights(0).wait()
    ahead(0)
    lax.fori_loop(0, cols - 1, one, 0)
    send(cols - 1)
    back(cols - 1)

    def results(members):
        for j in members:
            g = next(i for i, m in enumerate(groups) if j in m)
            rows = dx_refs[g].shape[0] // len(groups[g])
            i = groups[g].index(j)
            source = xt.at[pl.ds(pl.multiple_of(offs_s[j], 16), rows), :]
            yield pltpu.make_async_copy(
                source, dx_refs[g].at[i * rows : (i + 1) * rows, :], dx_sem.at[j]
            )

    per_set = blocks // len(sets)
    for members in sets:
        first = offs_s[members[0]]
        for j in members[1:]:
            first = jnp.minimum(first, offs_s[j])
        first = first // side

        def turn_back(i, carry):
            r = first + i
            xt[block(r), :] = acc[r].astype(xt.dtype)
            return carry

        lax.fori_loop(0, per_set, turn_back, 0, unroll=3)
        for copy in results(members):
            copy.start()

    def drain(c, carry):
        for copy in outs(c):
            copy.wait()
        return carry

    lax.fori_loop(0, cols, drain, 0)
    for members in sets:
        for copy in results(members):
            copy.wait()


def anywhere(count):
    return [pl.BlockSpec(memory_space=pl.ANY)] * count


def forward(shards, offs, weights, rows, cot, groups, sets):
    cols, slots, side, _ = weights.shape
    tokens = shards[0].shape[1]
    features = sum(s.shape[0] for s in shards)
    blocks = features // side
    part = shards[0].shape[0]
    flops = 4 * tokens * cols * slots * side * side
    dma = pltpu.SemaphoreType.DMA
    return pl.pallas_call(
        functools.partial(forward_kernel, len(shards), groups, sets),
        grid_spec=pltpu.PrefetchScalarGridSpec(
            num_scalar_prefetch=2,
            in_specs=anywhere(len(shards) + 2),
            out_specs=anywhere(2 + len(groups)),
            scratch_shapes=[
                pltpu.VMEM((features, tokens), jnp.bfloat16),
                pltpu.VMEM((blocks, tokens, side), jnp.bfloat16),
                pltpu.VMEM((blocks, tokens, side), jnp.float32),
                pltpu.VMEM(weights.shape, jnp.bfloat16),
                pltpu.VMEM((tokens, cols * side), jnp.bfloat16),
                pltpu.VMEM((cols, tokens, side), jnp.bfloat16),
                pltpu.VMEM((cols, tokens, side), jnp.bfloat16),
                dma((len(shards),)),
                dma((cols,)),
                dma,
                dma((2, cols)),
                dma((len(shards),)),
            ],
        ),
        out_shape=[jax.ShapeDtypeStruct((tokens, cols * side), jnp.bfloat16)] * 2
        + [jax.ShapeDtypeStruct((len(g) * part, tokens), jnp.bfloat16) for g in groups],
        compiler_params=pltpu.CompilerParams(vmem_limit_bytes=40 << 20),
        cost_estimate=pl.CostEstimate(
            flops=flops, bytes_accessed=2 * weights.size, transcendentals=tokens * cols * side
        ),
        name="forward",
    )(rows, offs, *shards, weights, cot)


def weight_kernel(n_planes, n_in, rows_s, offs_s, half_s, *refs):
    x_refs, refs = refs[: n_planes * n_in], refs[n_planes * n_in :]
    slope_refs, (out_ref, xt, slopes, out, x_sem, slope_sem, out_sem) = (
        refs[:n_planes],
        refs[n_planes:],
    )
    cols, slots, side, _ = out.shape
    tokens = slopes.shape[0] // n_planes

    def shard(p, j):
        ref = x_refs[p * n_in + j]
        rows = pl.ds(pl.multiple_of(offs_s[j], 16), ref.shape[0])
        target = xt.at[rows, p * tokens : (p + 1) * tokens]
        return pltpu.make_async_copy(ref, target, x_sem.at[p * n_in + j])

    def slope(p):
        target = slopes.at[p * tokens : (p + 1) * tokens, :]
        return pltpu.make_async_copy(slope_refs[p], target, slope_sem.at[p])

    def result(c):
        return pltpu.make_async_copy(out.at[c], out_ref.at[c], out_sem.at[c])

    copies = [shard(p, j) for p in range(n_planes) for j in range(n_in)]
    copies += [slope(p) for p in range(n_planes)]
    for copy in copies:
        copy.start()
    for copy in copies:
        copy.wait()

    def one(c, carry):
        right = slopes[:, pl.ds(pl.multiple_of(c * side, side), side)]
        for k in range(slots):
            r = rows_s[c, half_s[0] * slots + k]
            left = xt[pl.ds(pl.multiple_of(r * side, side), side), :]
            out[c, k] = jnp.dot(left, right, preferred_element_type=jnp.float32)
        result(c).start()
        return carry

    lax.fori_loop(0, cols, one, 0)

    def drain(c, carry):
        result(c).wait()
        return carry

    lax.fori_loop(0, cols, drain, 0)


def weight_grad(planes, offs, slopes, rows, half, slots, side):
    cols = rows.shape[0]
    tokens = slopes[0].shape[0]
    features = sum(s.shape[0] for s in planes[0])
    shards = [s for plane in planes for s in plane]
    dma = pltpu.SemaphoreType.DMA
    return pl.pallas_call(
        functools.partial(weight_kernel, len(planes), len(planes[0])),
        grid_spec=pltpu.PrefetchScalarGridSpec(
            num_scalar_prefetch=3,
            in_specs=anywhere(len(shards) + len(slopes)),
            out_specs=pl.BlockSpec(memory_space=pl.ANY),
            scratch_shapes=[
                pltpu.VMEM((features, len(planes) * tokens), jnp.bfloat16),
                pltpu.VMEM((len(planes) * tokens, cols * side), jnp.bfloat16),
                pltpu.VMEM((cols, slots, side, side), jnp.float32),
                dma((len(shards),)),
                dma((len(planes),)),
                dma((cols,)),
            ],
        ),
        out_shape=jax.ShapeDtypeStruct((cols, slots, side, side), jnp.float32),
        compiler_params=pltpu.CompilerParams(vmem_limit_bytes=40 << 20),
        cost_estimate=pl.CostEstimate(
            flops=2 * len(planes) * tokens * cols * slots * side * side,
            bytes_accessed=4 * cols * slots * side * side,
            transcendentals=0,
        ),
        name="weight_grad",
    )(rows, offs, half, *shards, *slopes)


def sum_kernel(sizes, *refs):
    refs = list(refs)
    ins, outs = refs[: sum(sizes)], refs[sum(sizes) :]
    for size, out in zip(sizes, outs):
        total = ins[0][...].astype(jnp.float32)
        for ref in ins[1:size]:
            total = total + ref[...].astype(jnp.float32)
        ins = ins[size:]
        out[...] = total.astype(out.dtype)


def add_parts(terms, part, tokens):
    flat = [t for group in terms for t in group]

    def spec(i):
        return pl.BlockSpec((part, tokens), lambda *_: (i, 0))

    return pl.pallas_call(
        functools.partial(sum_kernel, [len(g) for g in terms]),
        grid=(1,),
        in_specs=[spec(i) for _, i in flat],
        out_specs=[spec(0) for _ in terms],
        out_shape=[jax.ShapeDtypeStruct((part, tokens), jnp.bfloat16) for _ in terms],
        name="add_parts",
    )(*[a for a, _ in flat])


def body(activations, block_values, block_rows, cotangent):
    n, mp = lax.axis_size("dp"), lax.axis_size("mp")
    me, half = lax.axis_index("dp"), lax.axis_index("mp")
    side, slot_count = block_values.shape[2], block_values.shape[1]
    own = activations.T
    part, tokens = own.shape
    half = half.astype(jnp.int32).reshape(1)
    chip = CORES * SIDES
    line = n // chip
    if not direct(n, mp):
        offs = jnp.zeros((1,), jnp.int32)
        x_own = lax.all_gather(own, "dp", axis=0, tiled=True)
        x_all = lax.all_gather(x_own, "mp", axis=0)
        gelu_out, slopes, dx = forward(
            [x_own], offs, block_values, block_rows, cotangent, [(0,)], [(0,)]
        )
        slopes_all = lax.all_gather(slopes, "mp", axis=0)
        block_grad = weight_grad(
            [[x_all[p]] for p in range(mp)],
            offs,
            [slopes_all[p] for p in range(mp)],
            block_rows,
            half,
            slot_count // mp,
            side,
        )
        dx = dx.astype(jnp.float32)
        dx = lax.psum_scatter(dx, "dp", scatter_dimension=0, tiled=True)
        return gelu_out, dx.astype(jnp.bfloat16).T, block_grad

    def permute(a, k, s, q):
        def source(i):
            z, x, core = i // chip, i // CORES % SIDES, i % CORES
            return ((z + k) % line * SIDES + (x ^ s)) * CORES + (core ^ q)

        return lax.ppermute(a, "dp", [(source(i), i) for i in range(n)])

    def across(a):
        return lax.ppermute(a, "mp", [(i, i ^ 1) for i in range(mp)])

    rel = [(k, s, q) for q in range(CORES) for k in range(line) for s in range(SIDES)]
    ks, ss, qs = (np.array(v, np.int32) for v in zip(*rel))
    z, x, core = me // chip, me // CORES % SIDES, me % CORES
    offs = (((z + ks) % line * SIDES + (x ^ ss)) * CORES + (core ^ qs)) * part
    offs = offs.astype(jnp.int32)

    got = {(k, 0, 0): permute(own, k, 0, 0) if k else own for k in range(line)}
    for k in range(line):
        got[k, 1, 0] = permute(got[k, 0, 0], 0, 1, 0)
    far = {(k, s, q): across(a) for (k, s, q), a in got.items()}
    for k, s, q in rel:
        if q:
            got[k, s, 1] = permute(got[k, s, 0], 0, 0, 1)
            far[k, s, 1] = permute(far[k, s, 0], 0, 0, 1)
    x_own = [got[key] for key in rel]
    x_far = [far[key] for key in rel]

    per_core = len(rel) // CORES
    groups = [tuple(range(q * per_core, (q + 1) * per_core)) for q in range(CORES)]
    sets = [tuple(range(i, len(rel), per_core)) for i in range(per_core)]
    if CORES * part % side:
        sets = [tuple(range(len(rel)))]
    gelu_out, slopes, dx_own, dx_core = forward(
        x_own, offs, block_values, block_rows, cotangent, groups, sets
    )
    slopes_far = across(slopes)
    dx_in = permute(dx_core, 0, 0, 1)

    def at(k, s):
        return rel.index((k, s, 0))

    chips = add_parts(
        [[(dx_own, at(k, 1)), (dx_in, at(k, 1))] for k in range(line)], part, tokens
    )
    pairs = [permute(a, 0, 1, 0) for a in chips]
    last = [(dx_own, at(0, 0)), (dx_in, at(0, 0)), (pairs[0], 0)]
    for k in range(1, line):
        (mine,) = add_parts(
            [[(dx_own, at(k, 0)), (dx_in, at(k, 0)), (pairs[k], 0)]], part, tokens
        )
        last.append((permute(mine, line - k, 0, 0), 0))
    (dx,) = add_parts([last], part, tokens)
    block_grad = weight_grad(
        [x_own, x_far], offs, [slopes, slopes_far], block_rows, half, slot_count // mp, side
    )
    return gelu_out, dx.T, block_grad


def direct(n, mp):
    return n % (CORES * SIDES) == 0 and n // (CORES * SIDES) <= MAX_LINE and mp == 2


def solution(mesh):
    in_specs = (P("mp", "dp"), P("dp", None, None, None), P("dp", None), P("mp", "dp"))
    out_specs = (P("mp", "dp"), P("mp", "dp"), P("dp", "mp", None, None))
    return jax.shard_map(body, mesh=mesh, in_specs=in_specs, out_specs=out_specs, check_vma=False)
```

```python
import functools

import jax
import jax.numpy as jnp
import numpy as np
from jax import lax
from jax.experimental import pallas as pl
from jax.experimental.pallas import tpu as pltpu
from jax.sharding import PartitionSpec as P

CORES = 2
SIDES = 2
MAX_LINE = 8


SQRT_2_PI = float(np.sqrt(2.0 / np.pi))
CUBIC = 0.044715

VMEM = pl.BlockSpec(memory_space=pltpu.VMEM)
HBM = pl.BlockSpec(memory_space=pltpu.HBM)
DMA = pltpu.SemaphoreType.DMA
MARGIN = 4 << 20
ROOM = 60 * 1024 * 1024


def grant(*shapes):
    return MARGIN + sum(int(np.prod(s)) * np.dtype(d).itemsize for s, d in shapes)


def shards_of(refs, part):
    for ref in refs:
        for i in range(ref.shape[0] // part):
            yield ref.at[i * part : (i + 1) * part, :]


def block(r, side):
    return pl.ds(pl.multiple_of(r * side, side), side)


def forward_kernel(n_in, n_out, part, rows_s, offs_s, *refs):
    x_refs, refs = refs[:n_in], refs[n_in:]
    w_ref, cot, gelu_ref, slopes = refs[:4]
    dx_refs, (xt, xs, acc, gelu, w, out_sem, w_sem) = refs[4 : 4 + n_out], refs[4 + n_out :]
    cols, slots, side, _ = w.shape
    blocks = xs.shape[0]

    def out(c):
        target = gelu_ref.at[:, block(c, side)]
        return pltpu.make_async_copy(gelu.at[c], target, out_sem.at[c])

    def weights(c):
        return pltpu.make_async_copy(w_ref.at[c], w.at[c], w_sem.at[c])

    def load(c, carry):
        weights(c).start()
        return carry

    lax.fori_loop(0, cols, load, 0)
    for j, shard in enumerate(shards_of(x_refs, part)):
        xt[pl.ds(pl.multiple_of(offs_s[j], 16), part), :] = shard[...]

    def turn(r, carry):
        xs[r] = xt[block(r, side), :].T
        acc[r] = jnp.zeros(acc.shape[1:], acc.dtype)
        return carry

    lax.fori_loop(0, blocks, turn, 0, unroll=4)
    step = 2 if slots % 2 == 0 else 1

    def ahead(c):
        v = 0.0
        for k in range(0, slots, step):
            picked = jnp.concatenate([xs[rows_s[c, k + i]] for i in range(step)], axis=1)
            right = w[c, k : k + step].reshape(step * side, side)
            v = v + jnp.dot(picked, right, preferred_element_type=jnp.float32)
        v2 = v * v
        t = jnp.tanh(SQRT_2_PI * (v + CUBIC * (v * v2)))
        half = 0.5 * (1.0 + t)
        gelu[c] = (v * half).astype(gelu.dtype)
        slope = half + (0.5 * v) * (1.0 - t * t) * (SQRT_2_PI * (1.0 + (3.0 * CUBIC) * v2))
        slope = cot[:, block(c, side)].astype(jnp.float32) * slope
        slopes[:, block(c, side)] = slope.astype(slopes.dtype)

    def back(c):
        turned = slopes[:, block(c, side)].T
        for k in range(0, slots, step):
            left = w[c, k : k + step].reshape(step * side, side)
            part_sum = jnp.dot(left, turned, preferred_element_type=jnp.float32)
            for i in range(step):
                acc[rows_s[c, k + i]] += part_sum[i * side : (i + 1) * side, :]

    def one(c, carry):
        out(c).start()
        weights(c + 1).wait()
        ahead(c + 1)
        back(c)
        return carry

    weights(0).wait()
    ahead(0)
    lax.fori_loop(0, cols - 1, one, 0)
    out(cols - 1).start()
    back(cols - 1)

    def narrow(r, carry):
        xt[block(r, side), :] = acc[r].astype(xt.dtype)
        return carry

    lax.fori_loop(0, blocks, narrow, 0, unroll=4)
    for j, shard in enumerate(shards_of(dx_refs, part)):
        shard[...] = xt[pl.ds(pl.multiple_of(offs_s[j], 16), part), :]

    def drain(c, carry):
        out(c).wait()
        return carry

    lax.fori_loop(0, cols, drain, 0)


def forward(arrays, part, offs, weights, rows, cot, outs):
    cols, _, side, _ = weights.shape
    tokens = arrays[0].shape[1]
    features = sum(a.shape[0] for a in arrays)
    blocks = features // side
    scratch = [
        ((features, tokens), jnp.bfloat16),
        ((blocks, tokens, side), jnp.bfloat16),
        ((blocks, side, tokens), jnp.float32),
        ((cols, tokens, side), jnp.bfloat16),
        (weights.shape, jnp.bfloat16),
    ]
    return pl.pallas_call(
        functools.partial(forward_kernel, len(arrays), len(outs), part),
        grid_spec=pltpu.PrefetchScalarGridSpec(
            num_scalar_prefetch=2,
            in_specs=[VMEM] * len(arrays) + [HBM, VMEM],
            out_specs=[HBM, VMEM] + [VMEM] * len(outs),
            scratch_shapes=[pltpu.VMEM(*s) for s in scratch] + [DMA((cols,))] * 2,
        ),
        out_shape=[jax.ShapeDtypeStruct((tokens, cols * side), jnp.bfloat16)] * 2
        + [jax.ShapeDtypeStruct((m * part, tokens), jnp.bfloat16) for m in outs],
        compiler_params=pltpu.CompilerParams(
            vmem_limit_bytes=max(grant(*scratch), min(ROOM - 2 * weights.size, 48 << 20))
        ),
        cost_estimate=pl.CostEstimate(
            flops=4 * tokens * weights.size,
            bytes_accessed=2 * weights.size,
            transcendentals=tokens * cols * side,
        ),
        name="forward",
    )(rows, offs, *arrays, weights, cot)


def weight_kernel(n_planes, n_in, part, rows_s, offs_s, half_s, *refs):
    x_refs, refs = refs[: n_planes * n_in], refs[n_planes * n_in :]
    slope_refs, (out_ref, xt, out, out_sem) = refs[:n_planes], refs[n_planes:]
    cols, slots, side, _ = out.shape
    tokens = slope_refs[0].shape[0]

    def result(c):
        return pltpu.make_async_copy(out.at[c], out_ref.at[c], out_sem.at[c])

    for p in range(n_planes):
        for j, shard in enumerate(shards_of(x_refs[p * n_in : (p + 1) * n_in], part)):
            rows = pl.ds(pl.multiple_of(offs_s[j], 16), part)
            xt[rows, p * tokens : (p + 1) * tokens] = shard[...]

    def one(c, carry):
        right = jnp.concatenate([ref[:, block(c, side)] for ref in slope_refs], axis=0)
        for k in range(slots):
            left = xt[block(rows_s[c, half_s[0] * slots + k], side), :]
            out[c, k] = jnp.dot(left, right, preferred_element_type=jnp.float32)
        result(c).start()
        return carry

    lax.fori_loop(0, cols, one, 0, unroll=4 if cols % 4 == 0 else 1)

    def drain(c, carry):
        result(c).wait()
        return carry

    lax.fori_loop(0, cols, drain, 0)


def weight_grad(planes, part, offs, slopes, rows, half, slots, side):
    cols = rows.shape[0]
    tokens = slopes[0].shape[0]
    features = sum(a.shape[0] for a in planes[0])
    arrays = [a for plane in planes for a in plane]
    scratch = [
        ((features, len(planes) * tokens), jnp.bfloat16),
        ((cols, slots, side, side), jnp.float32),
    ]
    return pl.pallas_call(
        functools.partial(weight_kernel, len(planes), len(planes[0]), part),
        grid_spec=pltpu.PrefetchScalarGridSpec(
            num_scalar_prefetch=3,
            in_specs=[VMEM] * (len(arrays) + len(slopes)),
            out_specs=HBM,
            scratch_shapes=[pltpu.VMEM(*s) for s in scratch] + [DMA((cols,))],
        ),
        out_shape=jax.ShapeDtypeStruct((cols, slots, side, side), jnp.float32),
        compiler_params=pltpu.CompilerParams(vmem_limit_bytes=grant(*scratch)),
        cost_estimate=pl.CostEstimate(
            flops=2 * len(planes) * tokens * cols * slots * side * side,
            bytes_accessed=4 * cols * slots * side * side,
            transcendentals=0,
        ),
        name="weight_grad",
    )(rows, offs, half, *arrays, *slopes)


def pack_kernel(*refs):
    out, start = refs[-1], 0
    for ref in refs[:-1]:
        out[start : start + ref.shape[0], :] = ref[...]
        start += ref.shape[0]


def pack(arrays):
    rows = sum(a.shape[0] for a in arrays)
    return pl.pallas_call(
        pack_kernel,
        in_specs=[VMEM] * len(arrays),
        out_specs=VMEM,
        out_shape=jax.ShapeDtypeStruct((rows, arrays[0].shape[1]), arrays[0].dtype),
        compiler_params=pltpu.CompilerParams(vmem_limit_bytes=MARGIN),
        name="pack",
    )(*arrays)


def sum_kernel(plan, part, n_in, *refs):
    ins, outs = refs[:n_in], refs[n_in:]
    for terms, out in zip(plan, outs):
        total = 0.0
        for a, i in terms:
            total = total + ins[a][i * part : (i + 1) * part, :].astype(jnp.float32)
        out[...] = total.astype(out.dtype)


def add_parts(arrays, plan, part):
    tokens = arrays[0].shape[1]
    return pl.pallas_call(
        functools.partial(sum_kernel, plan, part, len(arrays)),
        in_specs=[VMEM] * len(arrays),
        out_specs=[VMEM] * len(plan),
        out_shape=[jax.ShapeDtypeStruct((part, tokens), jnp.bfloat16)] * len(plan),
        compiler_params=pltpu.CompilerParams(vmem_limit_bytes=MARGIN),
        name="add_parts",
    )(*arrays)


def direct(n, mp):
    return n % (CORES * SIDES) == 0 and n // (CORES * SIDES) <= MAX_LINE and mp == 2


def body(activations, block_values, block_rows, cotangent):
    n, mp = lax.axis_size("dp"), lax.axis_size("mp")
    me, half = lax.axis_index("dp"), lax.axis_index("mp")
    side, slot_count = block_values.shape[2], block_values.shape[1]
    own = activations.T
    part, _ = own.shape
    half = half.astype(jnp.int32).reshape(1)
    chip = CORES * SIDES
    line = n // chip
    if not direct(n, mp):
        offs = jnp.zeros((1,), jnp.int32)
        x_own = lax.all_gather(own, "dp", axis=0, tiled=True)
        x_all = lax.all_gather(x_own, "mp", axis=0)
        whole = x_own.shape[0]
        gelu_out, slopes, dx = forward(
            [x_own], whole, offs, block_values, block_rows, cotangent, [1]
        )
        slopes_all = lax.all_gather(slopes, "mp", axis=0)
        block_grad = weight_grad(
            [[x_all[p]] for p in range(mp)],
            whole,
            offs,
            [slopes_all[p] for p in range(mp)],
            block_rows,
            half,
            slot_count // mp,
            side,
        )
        dx = dx.astype(jnp.float32)
        dx = lax.psum_scatter(dx, "dp", scatter_dimension=0, tiled=True)
        return gelu_out, dx.astype(jnp.bfloat16).T, block_grad

    def permute(a, k, s, q):
        def source(i):
            z, x, core = i // chip, i // CORES % SIDES, i % CORES
            return ((z + k) % line * SIDES + (x ^ s)) * CORES + (core ^ q)

        return lax.ppermute(a, "dp", [(source(i), i) for i in range(n)])

    def across(a):
        return lax.ppermute(a, "mp", [(i, i ^ 1) for i in range(mp)])

    rel = [(k, s, q) for q in range(CORES) for s in range(SIDES) for k in range(line)]
    ks, ss, qs = (np.array(v, np.int32) for v in zip(*rel))
    z, x, core = me // chip, me // CORES % SIDES, me % CORES
    offs = (((z + ks) % line * SIDES + (x ^ ss)) * CORES + (core ^ qs)) * part
    offs = offs.astype(jnp.int32)

    near = [permute(own, k, 0, 0) if k else own for k in range(line)]
    side_x = [permute(a, 0, 1, 0) for a in near]
    x_own, x_far = [], []
    for s, arrays in enumerate((near, side_x)):
        x_own.append(pack(arrays))
        x_far.append(across(x_own[s]))
    for s in range(SIDES):
        x_own.append(permute(x_own[s], 0, 0, 1))
        x_far.append(permute(x_far[s], 0, 0, 1))

    gelu_out, slopes, keep0, keep1, give0, give1 = forward(
        x_own, part, offs, block_values, block_rows, cotangent, [line] * 4
    )
    got1 = permute(give1, 0, 0, 1)
    got0 = permute(give0, 0, 0, 1)
    slopes_far = across(slopes)
    chips = add_parts([keep1, got1], [[(0, k), (1, k)] for k in range(line)], part)
    pairs = [permute(a, 0, 1, 0) for a in chips]
    total = (
        keep0[:part].astype(jnp.float32)
        + got0[:part].astype(jnp.float32)
        + pairs[0].astype(jnp.float32)
    )
    for k in range(1, line):
        (mine,) = add_parts([keep0, got0, pairs[k]], [[(0, k), (1, k), (2, 0)]], part)
        total = total + permute(mine, line - k, 0, 0).astype(jnp.float32)
    block_grad = weight_grad(
        [x_own, x_far],
        part,
        offs,
        [slopes, slopes_far],
        block_rows,
        half,
        slot_count // mp,
        side,
    )
    return gelu_out, total.astype(jnp.bfloat16).T, block_grad


def solution(mesh):
    in_specs = (P("mp", "dp"), P("dp", None, None, None), P("dp", None), P("mp", "dp"))
    out_specs = (P("mp", "dp"), P("mp", "dp"), P("dp", "mp", None, None))
    return jax.shard_map(
        body, mesh=mesh, in_specs=in_specs, out_specs=out_specs, check_vma=False
    )
```

```python
import functools

import jax
import jax.numpy as jnp
import numpy as np
from jax import lax
from jax.experimental import pallas as pl
from jax.experimental.pallas import tpu as pltpu
from jax.sharding import PartitionSpec as P

CORES = 2
SIDES = 2
MAX_LINE = 8


SQRT_2_PI = float(np.sqrt(2.0 / np.pi))
CUBIC = 0.044715

VMEM = pl.BlockSpec(memory_space=pltpu.VMEM)
HBM = pl.BlockSpec(memory_space=pltpu.HBM)
DMA = pltpu.SemaphoreType.DMA
MARGIN = 4 << 20
ROOM = 60 * 1024 * 1024


def grant(*shapes):
    return MARGIN + sum(int(np.prod(s)) * np.dtype(d).itemsize for s, d in shapes)


def shards_of(refs, part):
    for ref in refs:
        for i in range(ref.shape[0] // part):
            yield ref.at[i * part : (i + 1) * part, :]


def block(r, side):
    return pl.ds(pl.multiple_of(r * side, side), side)


def forward_kernel(n_in, n_out, part, rows_s, offs_s, *refs):
    x_refs, refs = refs[:n_in], refs[n_in:]
    w_ref, cot, gelu_ref, slopes = refs[:4]
    dx_refs, (xt, xs, acc, gelu, w, out_sem, w_sem) = refs[4 : 4 + n_out], refs[4 + n_out :]
    cols, slots, side, _ = w.shape
    blocks = xs.shape[0]

    def out(c):
        target = gelu_ref.at[:, block(c, side)]
        return pltpu.make_async_copy(gelu.at[c], target, out_sem.at[c])

    def weights(c):
        return pltpu.make_async_copy(w_ref.at[c], w.at[c], w_sem.at[c])

    def load(c, carry):
        weights(c).start()
        return carry

    lax.fori_loop(0, cols, load, 0)
    for j, shard in enumerate(shards_of(x_refs, part)):
        xt[pl.ds(pl.multiple_of(offs_s[j], 16), part), :] = shard[...]

    def turn(r, carry):
        xs[r] = xt[block(r, side), :].T
        acc[block(r, side), :] = jnp.zeros((side, acc.shape[1]), acc.dtype)
        return carry

    lax.fori_loop(0, blocks, turn, 0, unroll=4)
    step = 2 if slots % 2 == 0 else 1

    def ahead(c):
        v = 0.0
        for k in range(0, slots, step):
            picked = jnp.concatenate([xs[rows_s[c, k + i]] for i in range(step)], axis=1)
            right = w[c, k : k + step].reshape(step * side, side)
            v = v + jnp.dot(picked, right, preferred_element_type=jnp.float32)
        v2 = v * v
        t = jnp.tanh(SQRT_2_PI * (v + CUBIC * (v * v2)))
        half = 0.5 * (1.0 + t)
        gelu[c] = (v * half).astype(gelu.dtype)
        slope = half + (0.5 * v) * (1.0 - t * t) * (SQRT_2_PI * (1.0 + (3.0 * CUBIC) * v2))
        slope = cot[:, block(c, side)].astype(jnp.float32) * slope
        slopes[:, block(c, side)] = slope.astype(slopes.dtype)

    def back(c):
        turned = slopes[:, block(c, side)].T
        for k in range(0, slots, step):
            left = w[c, k : k + step].reshape(step * side, side)
            part_sum = jnp.dot(left, turned, preferred_element_type=jnp.float32)
            for i in range(step):
                acc[block(rows_s[c, k + i], side), :] += part_sum[i * side : (i + 1) * side]

    def one(c, carry):
        out(c).start()
        weights(c + 1).wait()
        ahead(c + 1)
        back(c)
        return carry

    weights(0).wait()
    ahead(0)
    lax.fori_loop(0, cols - 1, one, 0)
    out(cols - 1).start()
    back(cols - 1)

    for j, shard in enumerate(shards_of(dx_refs, part)):
        rows = pl.ds(pl.multiple_of(offs_s[j], 16), part)
        shard[...] = acc[rows, :].astype(shard.dtype)

    def drain(c, carry):
        out(c).wait()
        return carry

    lax.fori_loop(0, cols, drain, 0)


def forward(arrays, part, offs, weights, rows, cot, outs):
    cols, _, side, _ = weights.shape
    tokens = arrays[0].shape[1]
    features = sum(a.shape[0] for a in arrays)
    blocks = features // side
    scratch = [
        ((features, tokens), jnp.bfloat16),
        ((blocks, tokens, side), jnp.bfloat16),
        ((features, tokens), jnp.float32),
        ((cols, tokens, side), jnp.bfloat16),
        (weights.shape, jnp.bfloat16),
    ]
    return pl.pallas_call(
        functools.partial(forward_kernel, len(arrays), len(outs), part),
        grid_spec=pltpu.PrefetchScalarGridSpec(
            num_scalar_prefetch=2,
            in_specs=[VMEM] * len(arrays) + [HBM, VMEM],
            out_specs=[HBM, VMEM] + [VMEM] * len(outs),
            scratch_shapes=[pltpu.VMEM(*s) for s in scratch] + [DMA((cols,))] * 2,
        ),
        out_shape=[jax.ShapeDtypeStruct((tokens, cols * side), jnp.bfloat16)] * 2
        + [jax.ShapeDtypeStruct((m * part, tokens), jnp.bfloat16) for m in outs],
        compiler_params=pltpu.CompilerParams(
            vmem_limit_bytes=max(grant(*scratch), min(ROOM - 2 * weights.size, 48 << 20))
        ),
        cost_estimate=pl.CostEstimate(
            flops=4 * tokens * weights.size,
            bytes_accessed=2 * weights.size,
            transcendentals=tokens * cols * side,
        ),
        name="forward",
    )(rows, offs, *arrays, weights, cot)


def weight_kernel(n_planes, n_in, part, rows_s, offs_s, half_s, *refs):
    x_refs, refs = refs[: n_planes * n_in], refs[n_planes * n_in :]
    slope_refs, (out_ref, xt, out, out_sem) = refs[:n_planes], refs[n_planes:]
    cols, slots, side, _ = out.shape
    tokens = slope_refs[0].shape[0]

    def result(c):
        return pltpu.make_async_copy(out.at[c], out_ref.at[c], out_sem.at[c])

    for p in range(n_planes):
        for j, shard in enumerate(shards_of(x_refs[p * n_in : (p + 1) * n_in], part)):
            rows = pl.ds(pl.multiple_of(offs_s[j], 16), part)
            xt[rows, p * tokens : (p + 1) * tokens] = shard[...]

    def one(c, carry):
        right = jnp.concatenate([ref[:, block(c, side)] for ref in slope_refs], axis=0)
        for k in range(slots):
            left = xt[block(rows_s[c, half_s[0] * slots + k], side), :]
            out[c, k] = jnp.dot(left, right, preferred_element_type=jnp.float32)
        result(c).start()
        return carry

    lax.fori_loop(0, cols, one, 0, unroll=4 if cols % 4 == 0 else 1)

    def drain(c, carry):
        result(c).wait()
        return carry

    lax.fori_loop(0, cols, drain, 0)


def weight_grad(planes, part, offs, slopes, rows, half, slots, side):
    cols = rows.shape[0]
    tokens = slopes[0].shape[0]
    features = sum(a.shape[0] for a in planes[0])
    arrays = [a for plane in planes for a in plane]
    scratch = [
        ((features, len(planes) * tokens), jnp.bfloat16),
        ((cols, slots, side, side), jnp.float32),
    ]
    return pl.pallas_call(
        functools.partial(weight_kernel, len(planes), len(planes[0]), part),
        grid_spec=pltpu.PrefetchScalarGridSpec(
            num_scalar_prefetch=3,
            in_specs=[VMEM] * (len(arrays) + len(slopes)),
            out_specs=HBM,
            scratch_shapes=[pltpu.VMEM(*s) for s in scratch] + [DMA((cols,))],
        ),
        out_shape=jax.ShapeDtypeStruct((cols, slots, side, side), jnp.float32),
        compiler_params=pltpu.CompilerParams(vmem_limit_bytes=grant(*scratch)),
        cost_estimate=pl.CostEstimate(
            flops=2 * len(planes) * tokens * cols * slots * side * side,
            bytes_accessed=4 * cols * slots * side * side,
            transcendentals=0,
        ),
        name="weight_grad",
    )(rows, offs, half, *arrays, *slopes)


def pack_kernel(*refs):
    out, start = refs[-1], 0
    for ref in refs[:-1]:
        out[start : start + ref.shape[0], :] = ref[...]
        start += ref.shape[0]


def pack(arrays):
    rows = sum(a.shape[0] for a in arrays)
    return pl.pallas_call(
        pack_kernel,
        in_specs=[VMEM] * len(arrays),
        out_specs=VMEM,
        out_shape=jax.ShapeDtypeStruct((rows, arrays[0].shape[1]), arrays[0].dtype),
        compiler_params=pltpu.CompilerParams(vmem_limit_bytes=MARGIN),
        name="pack",
    )(*arrays)


def stage_kernel(*refs):
    half = len(refs) // 2
    for source, target in zip(refs[:half], refs[half:]):
        target[...] = source[...]


def stage(*arrays):
    return pl.pallas_call(
        stage_kernel,
        in_specs=[VMEM] * len(arrays),
        out_specs=[VMEM] * len(arrays),
        out_shape=[jax.ShapeDtypeStruct(a.shape, a.dtype) for a in arrays],
        compiler_params=pltpu.CompilerParams(vmem_limit_bytes=MARGIN),
        name="stage",
    )(*arrays)


def sum_kernel(plan, part, n_in, *refs):
    ins, outs = refs[:n_in], refs[n_in:]
    for terms, out in zip(plan, outs):
        total = 0.0
        for a, i in terms:
            total = total + ins[a][i * part : (i + 1) * part, :].astype(jnp.float32)
        out[...] = total.astype(out.dtype)


def add_parts(arrays, plan, part):
    tokens = arrays[0].shape[1]
    return pl.pallas_call(
        functools.partial(sum_kernel, plan, part, len(arrays)),
        in_specs=[VMEM] * len(arrays),
        out_specs=[VMEM] * len(plan),
        out_shape=[jax.ShapeDtypeStruct((part, tokens), jnp.bfloat16)] * len(plan),
        compiler_params=pltpu.CompilerParams(vmem_limit_bytes=MARGIN),
        name="add_parts",
    )(*arrays)


def direct(n, mp):
    return n % (CORES * SIDES) == 0 and 2 <= n // (CORES * SIDES) <= MAX_LINE and mp == 2


def body(activations, block_values, block_rows, cotangent):
    n, mp = lax.axis_size("dp"), lax.axis_size("mp")
    me, half = lax.axis_index("dp"), lax.axis_index("mp")
    side, slot_count = block_values.shape[2], block_values.shape[1]
    own = activations.T
    part, _ = own.shape
    half = half.astype(jnp.int32).reshape(1)
    chip = CORES * SIDES
    line = n // chip
    if not direct(n, mp):
        offs = jnp.zeros((1,), jnp.int32)
        x_own = lax.all_gather(own, "dp", axis=0, tiled=True)
        x_all = lax.all_gather(x_own, "mp", axis=0)
        whole = x_own.shape[0]
        gelu_out, slopes, dx = forward(
            [x_own], whole, offs, block_values, block_rows, cotangent, [1]
        )
        slopes_all = lax.all_gather(slopes, "mp", axis=0)
        block_grad = weight_grad(
            [[x_all[p]] for p in range(mp)],
            whole,
            offs,
            [slopes_all[p] for p in range(mp)],
            block_rows,
            half,
            slot_count // mp,
            side,
        )
        dx = dx.astype(jnp.float32)
        dx = lax.psum_scatter(dx, "dp", scatter_dimension=0, tiled=True)
        return gelu_out, dx.astype(jnp.bfloat16).T, block_grad

    def along(z, k):
        return z ^ k if line & (line - 1) == 0 else (z + k) % line

    def permute(a, k, s, q):
        def source(i):
            z, x, core = i // chip, i // CORES % SIDES, i % CORES
            return (along(z, k) * SIDES + (x ^ s)) * CORES + (core ^ q)

        return lax.ppermute(a, "dp", [(source(i), i) for i in range(n)])

    def back_to(k):
        return next(i for i in range(line) if along(along(0, k), i) == 0)

    def across(a):
        return lax.ppermute(a, "mp", [(i, i ^ 1) for i in range(mp)])

    rel = [(k, s, q) for q in range(CORES) for s in range(SIDES) for k in range(line)]
    ks, ss, qs = (np.array(v, np.int32) for v in zip(*rel))
    z, x, core = me // chip, me // CORES % SIDES, me % CORES
    offs = ((along(z, ks) * SIDES + (x ^ ss)) * CORES + (core ^ qs)) * part
    offs = offs.astype(jnp.int32)

    cotangent, block_rows = stage(cotangent, block_rows)
    near = [permute(own, k, 0, 0) if k else own for k in range(line)]
    side_x = [permute(a, 0, 1, 0) for a in near]
    x_own, x_far = [], []
    for s, arrays in enumerate((near, side_x)):
        x_own.append(pack(arrays))
        x_far.append(across(x_own[s]))
    for s in range(SIDES):
        x_own.append(permute(x_own[s], 0, 0, 1))
        x_far.append(permute(x_far[s], 0, 0, 1))

    gelu_out, slopes, keep0, keep1, give0, give1 = forward(
        x_own, part, offs, block_values, block_rows, cotangent, [line] * 4
    )
    got1 = permute(give1, 0, 0, 1)
    got0 = permute(give0, 0, 0, 1)
    slopes_far = across(slopes)
    first = add_parts([keep1, got1], [[(0, k), (1, k)] for k in range(1, line)], part)
    chips = add_parts([keep1, got1], [[(0, 0), (1, 0)]], part) + first
    pairs = [permute(a, 0, 1, 0) for a in chips]
    total = (
        keep0[:part].astype(jnp.float32)
        + got0[:part].astype(jnp.float32)
        + pairs[0].astype(jnp.float32)
    )
    for k in range(1, line):
        (mine,) = add_parts([keep0, got0, pairs[k]], [[(0, k), (1, k), (2, 0)]], part)
        total = total + permute(mine, back_to(k), 0, 0).astype(jnp.float32)
    block_grad = weight_grad(
        [x_own, x_far],
        part,
        offs,
        [slopes, slopes_far],
        block_rows,
        half,
        slot_count // mp,
        side,
    )
    return gelu_out, total.astype(jnp.bfloat16).T, block_grad


def solution(mesh):
    in_specs = (P("mp", "dp"), P("dp", None, None, None), P("dp", None), P("mp", "dp"))
    out_specs = (P("mp", "dp"), P("mp", "dp"), P("dp", "mp", None, None))
    step = jax.shard_map(body, mesh=mesh, in_specs=in_specs, out_specs=out_specs, check_vma=False)
    n, mp = mesh.shape["dp"], mesh.shape["mp"]
    if not direct(n, mp):
        return step
    return step
```

```python
import functools

import jax
import jax.numpy as jnp
import numpy as np
from jax import lax
from jax.experimental import pallas as pl
from jax.experimental.pallas import tpu as pltpu
from jax.sharding import PartitionSpec as P

CORES = 2
SIDES = 2
MAX_LINE = 8


SQRT_2_PI = float(np.sqrt(2.0 / np.pi))
CUBIC = 0.044715

VMEM = pl.BlockSpec(memory_space=pltpu.VMEM)
HBM = pl.BlockSpec(memory_space=pltpu.HBM)
DMA = pltpu.SemaphoreType.DMA
MARGIN = 4 << 20
ROOM = 60 * 1024 * 1024


def grant(*shapes):
    return MARGIN + sum(int(np.prod(s)) * np.dtype(d).itemsize for s, d in shapes)


def shards_of(refs, part):
    for ref in refs:
        for i in range(ref.shape[0] // part):
            yield ref.at[i * part : (i + 1) * part, :]


def block(r, side):
    return pl.ds(pl.multiple_of(r * side, side), side)


def forward_kernel(n_in, n_out, part, rows_s, offs_s, *refs):
    x_refs, refs = refs[:n_in], refs[n_in:]
    w_ref, cot, gelu_ref, slopes = refs[:4]
    dx_refs, (xt, xs, acc, gelu, w, out_sem, w_sem) = refs[4 : 4 + n_out], refs[4 + n_out :]
    cols, slots, side, _ = w.shape
    blocks = xs.shape[0]

    def out(c):
        target = gelu_ref.at[:, block(c, side)]
        return pltpu.make_async_copy(gelu.at[c], target, out_sem.at[c])

    def weights(c):
        return pltpu.make_async_copy(w_ref.at[c], w.at[c], w_sem.at[c])

    def load(c, carry):
        weights(c).start()
        return carry

    lax.fori_loop(0, cols, load, 0)
    for j, shard in enumerate(shards_of(x_refs, part)):
        xt[pl.ds(pl.multiple_of(offs_s[j], 16), part), :] = shard[...]

    def turn(r, carry):
        xs[r] = xt[block(r, side), :].T
        acc[block(r, side), :] = jnp.zeros((side, acc.shape[1]), acc.dtype)
        return carry

    lax.fori_loop(0, blocks, turn, 0, unroll=4)
    step = 2 if slots % 2 == 0 else 1

    def activate(c, v):
        v2 = v * v
        t = jnp.tanh(SQRT_2_PI * (v + CUBIC * (v * v2)))
        half = 0.5 * (1.0 + t)
        gelu[c] = (v * half).astype(gelu.dtype)
        slope = half + (0.5 * v) * (1.0 - t * t) * (SQRT_2_PI * (1.0 + (3.0 * CUBIC) * v2))
        slope = cot[:, block(c, side)].astype(jnp.float32) * slope
        slopes[:, block(c, side)] = slope.astype(slopes.dtype)

    def ahead(c, k):
        picked = jnp.concatenate([xs[rows_s[c, k + i]] for i in range(step)], axis=1)
        right = w[c, k : k + step].reshape(step * side, side)
        return jnp.dot(picked, right, preferred_element_type=jnp.float32)

    def back(c, k, turned):
        left = w[c, k : k + step].reshape(step * side, side)
        part_sum = jnp.dot(left, turned, preferred_element_type=jnp.float32)
        for i in range(step):
            acc[block(rows_s[c, k + i], side), :] += part_sum[i * side : (i + 1) * side]

    def one(c, carry):
        out(c).start()
        weights(c + 1).wait()
        turned = slopes[:, block(c, side)].T
        v = 0.0
        for k in range(0, slots, step):
            v = v + ahead(c + 1, k)
            back(c, k, turned)
        activate(c + 1, v)
        return carry

    weights(0).wait()
    activate(0, sum(ahead(0, k) for k in range(0, slots, step)))
    lax.fori_loop(0, cols - 1, one, 0)
    out(cols - 1).start()
    turned = slopes[:, block(cols - 1, side)].T
    for k in range(0, slots, step):
        back(cols - 1, k, turned)

    for j, shard in enumerate(shards_of(dx_refs, part)):
        rows = pl.ds(pl.multiple_of(offs_s[j], 16), part)
        shard[...] = acc[rows, :].astype(shard.dtype)

    def drain(c, carry):
        out(c).wait()
        return carry

    lax.fori_loop(0, cols, drain, 0)


def forward(arrays, part, offs, weights, rows, cot, outs):
    cols, _, side, _ = weights.shape
    tokens = arrays[0].shape[1]
    features = sum(a.shape[0] for a in arrays)
    blocks = features // side
    scratch = [
        ((features, tokens), jnp.bfloat16),
        ((blocks, tokens, side), jnp.bfloat16),
        ((features, tokens), jnp.float32),
        ((cols, tokens, side), jnp.bfloat16),
        (weights.shape, jnp.bfloat16),
    ]
    return pl.pallas_call(
        functools.partial(forward_kernel, len(arrays), len(outs), part),
        grid_spec=pltpu.PrefetchScalarGridSpec(
            num_scalar_prefetch=2,
            in_specs=[VMEM] * len(arrays) + [HBM, VMEM],
            out_specs=[HBM, VMEM] + [VMEM] * len(outs),
            scratch_shapes=[pltpu.VMEM(*s) for s in scratch] + [DMA((cols,))] * 2,
        ),
        out_shape=[jax.ShapeDtypeStruct((tokens, cols * side), jnp.bfloat16)] * 2
        + [jax.ShapeDtypeStruct((m * part, tokens), jnp.bfloat16) for m in outs],
        compiler_params=pltpu.CompilerParams(
            vmem_limit_bytes=max(grant(*scratch), min(ROOM - 2 * weights.size, 48 << 20))
        ),
        cost_estimate=pl.CostEstimate(
            flops=4 * tokens * weights.size,
            bytes_accessed=2 * weights.size,
            transcendentals=tokens * cols * side,
        ),
        name="forward",
    )(rows, offs, *arrays, weights, cot)


def weight_kernel(n_planes, n_in, part, rows_s, offs_s, half_s, *refs):
    x_refs, refs = refs[: n_planes * n_in], refs[n_planes * n_in :]
    slope_refs, (out_ref, xt, out, out_sem) = refs[:n_planes], refs[n_planes:]
    cols, slots, side, _ = out.shape
    tokens = slope_refs[0].shape[0]

    def result(c):
        return pltpu.make_async_copy(out.at[c], out_ref.at[c], out_sem.at[c])

    for p in range(n_planes):
        for j, shard in enumerate(shards_of(x_refs[p * n_in : (p + 1) * n_in], part)):
            rows = pl.ds(pl.multiple_of(offs_s[j], 16), part)
            xt[rows, p * tokens : (p + 1) * tokens] = shard[...]

    def one(c, carry):
        right = jnp.concatenate([ref[:, block(c, side)] for ref in slope_refs], axis=0)
        for k in range(slots):
            left = xt[block(rows_s[c, half_s[0] * slots + k], side), :]
            out[c, k] = jnp.dot(left, right, preferred_element_type=jnp.float32)
        result(c).start()
        return carry

    lax.fori_loop(0, cols, one, 0, unroll=4 if cols % 4 == 0 else 1)

    def drain(c, carry):
        result(c).wait()
        return carry

    lax.fori_loop(0, cols, drain, 0)


def weight_grad(planes, part, offs, slopes, rows, half, slots, side):
    cols = rows.shape[0]
    tokens = slopes[0].shape[0]
    features = sum(a.shape[0] for a in planes[0])
    arrays = [a for plane in planes for a in plane]
    scratch = [
        ((features, len(planes) * tokens), jnp.bfloat16),
        ((cols, slots, side, side), jnp.float32),
    ]
    return pl.pallas_call(
        functools.partial(weight_kernel, len(planes), len(planes[0]), part),
        grid_spec=pltpu.PrefetchScalarGridSpec(
            num_scalar_prefetch=3,
            in_specs=[VMEM] * (len(arrays) + len(slopes)),
            out_specs=HBM,
            scratch_shapes=[pltpu.VMEM(*s) for s in scratch] + [DMA((cols,))],
        ),
        out_shape=jax.ShapeDtypeStruct((cols, slots, side, side), jnp.float32),
        compiler_params=pltpu.CompilerParams(vmem_limit_bytes=grant(*scratch)),
        cost_estimate=pl.CostEstimate(
            flops=2 * len(planes) * tokens * cols * slots * side * side,
            bytes_accessed=4 * cols * slots * side * side,
            transcendentals=0,
        ),
        name="weight_grad",
    )(rows, offs, half, *arrays, *slopes)


def pack_kernel(*refs):
    out, start = refs[-1], 0
    for ref in refs[:-1]:
        out[start : start + ref.shape[0], :] = ref[...]
        start += ref.shape[0]


def pack(arrays):
    rows = sum(a.shape[0] for a in arrays)
    return pl.pallas_call(
        pack_kernel,
        in_specs=[VMEM] * len(arrays),
        out_specs=VMEM,
        out_shape=jax.ShapeDtypeStruct((rows, arrays[0].shape[1]), arrays[0].dtype),
        compiler_params=pltpu.CompilerParams(vmem_limit_bytes=MARGIN),
        name="pack",
    )(*arrays)


def stage_kernel(*refs):
    half = len(refs) // 2
    for source, target in zip(refs[:half], refs[half:]):
        target[...] = source[...]


def stage(*arrays):
    return pl.pallas_call(
        stage_kernel,
        in_specs=[VMEM] * len(arrays),
        out_specs=[VMEM] * len(arrays),
        out_shape=[jax.ShapeDtypeStruct(a.shape, a.dtype) for a in arrays],
        compiler_params=pltpu.CompilerParams(vmem_limit_bytes=MARGIN),
        name="stage",
    )(*arrays)


def sum_kernel(plan, part, n_in, *refs):
    ins, outs = refs[:n_in], refs[n_in:]
    for terms, out in zip(plan, outs):
        total = 0.0
        for a, i in terms:
            total = total + ins[a][i * part : (i + 1) * part, :].astype(jnp.float32)
        out[...] = total.astype(out.dtype)


def add_parts(arrays, plan, part):
    tokens = arrays[0].shape[1]
    return pl.pallas_call(
        functools.partial(sum_kernel, plan, part, len(arrays)),
        in_specs=[VMEM] * len(arrays),
        out_specs=[VMEM] * len(plan),
        out_shape=[jax.ShapeDtypeStruct((part, tokens), jnp.bfloat16)] * len(plan),
        compiler_params=pltpu.CompilerParams(vmem_limit_bytes=MARGIN),
        name="add_parts",
    )(*arrays)


def direct(n, mp):
    return n % (CORES * SIDES) == 0 and 2 <= n // (CORES * SIDES) <= MAX_LINE and mp == 2


def body(activations, block_values, block_rows, cotangent):
    n, mp = lax.axis_size("dp"), lax.axis_size("mp")
    me, half = lax.axis_index("dp"), lax.axis_index("mp")
    side, slot_count = block_values.shape[2], block_values.shape[1]
    own = activations.T
    part, _ = own.shape
    half = half.astype(jnp.int32).reshape(1)
    chip = CORES * SIDES
    line = n // chip
    if not direct(n, mp):
        offs = jnp.zeros((1,), jnp.int32)
        x_own = lax.all_gather(own, "dp", axis=0, tiled=True)
        x_all = lax.all_gather(x_own, "mp", axis=0)
        whole = x_own.shape[0]
        gelu_out, slopes, dx = forward(
            [x_own], whole, offs, block_values, block_rows, cotangent, [1]
        )
        slopes_all = lax.all_gather(slopes, "mp", axis=0)
        block_grad = weight_grad(
            [[x_all[p]] for p in range(mp)],
            whole,
            offs,
            [slopes_all[p] for p in range(mp)],
            block_rows,
            half,
            slot_count // mp,
            side,
        )
        dx = dx.astype(jnp.float32)
        dx = lax.psum_scatter(dx, "dp", scatter_dimension=0, tiled=True)
        return gelu_out, dx.astype(jnp.bfloat16).T, block_grad

    def along(z, k):
        return z ^ k if line & (line - 1) == 0 else (z + k) % line

    def permute(a, k, s, q):
        def source(i):
            z, x, core = i // chip, i // CORES % SIDES, i % CORES
            return (along(z, k) * SIDES + (x ^ s)) * CORES + (core ^ q)

        return lax.ppermute(a, "dp", [(source(i), i) for i in range(n)])

    def back_to(k):
        return next(i for i in range(line) if along(along(0, k), i) == 0)

    def across(a):
        return lax.ppermute(a, "mp", [(i, i ^ 1) for i in range(mp)])

    rel = [(k, s, q) for q in range(CORES) for s in range(SIDES) for k in range(line)]
    ks, ss, qs = (np.array(v, np.int32) for v in zip(*rel))
    z, x, core = me // chip, me // CORES % SIDES, me % CORES
    offs = ((along(z, ks) * SIDES + (x ^ ss)) * CORES + (core ^ qs)) * part
    offs = offs.astype(jnp.int32)

    cotangent, block_rows = stage(cotangent, block_rows)
    near = [permute(own, k, 0, 0) if k else own for k in range(line)]
    side_x = [permute(a, 0, 1, 0) for a in near]
    x_own, x_far = [], []
    for s, arrays in enumerate((near, side_x)):
        x_own.append(pack(arrays))
        x_far.append(across(x_own[s]))
    for s in range(SIDES):
        x_own.append(permute(x_own[s], 0, 0, 1))
        x_far.append(permute(x_far[s], 0, 0, 1))

    gelu_out, slopes, keep0, keep1, give0, give1 = forward(
        x_own, part, offs, block_values, block_rows, cotangent, [line] * 4
    )
    got1 = permute(give1, 0, 0, 1)
    got0 = permute(give0, 0, 0, 1)
    slopes_far = across(slopes)
    first = add_parts([keep1, got1], [[(0, k), (1, k)] for k in range(1, line)], part)
    chips = add_parts([keep1, got1], [[(0, 0), (1, 0)]], part) + first
    pairs = [permute(a, 0, 1, 0) for a in chips]
    total = (
        keep0[:part].astype(jnp.float32)
        + got0[:part].astype(jnp.float32)
        + pairs[0].astype(jnp.float32)
    )
    for k in range(1, line):
        (mine,) = add_parts([keep0, got0, pairs[k]], [[(0, k), (1, k), (2, 0)]], part)
        total = total + permute(mine, back_to(k), 0, 0).astype(jnp.float32)
    block_grad = weight_grad(
        [x_own, x_far],
        part,
        offs,
        [slopes, slopes_far],
        block_rows,
        half,
        slot_count // mp,
        side,
    )
    return gelu_out, total.astype(jnp.bfloat16).T, block_grad


def solution(mesh):
    in_specs = (P("mp", "dp"), P("dp", None, None, None), P("dp", None), P("mp", "dp"))
    out_specs = (P("mp", "dp"), P("mp", "dp"), P("dp", "mp", None, None))
    step = jax.shard_map(
        body, mesh=mesh, in_specs=in_specs, out_specs=out_specs, check_vma=False
    )
    n, mp = mesh.shape["dp"], mesh.shape["mp"]
    if not direct(n, mp):
        return step
    return step
```

```python
import functools

import jax
import jax.numpy as jnp
import numpy as np
from jax import lax
from jax.experimental import pallas as pl
from jax.experimental.pallas import tpu as pltpu
from jax.sharding import PartitionSpec as P

CORES = 2
SIDES = 2
MAX_LINE = 8


SQRT_2_PI = float(np.sqrt(2.0 / np.pi))
CUBIC = 0.044715

VMEM = pl.BlockSpec(memory_space=pltpu.VMEM)
HBM = pl.BlockSpec(memory_space=pltpu.HBM)
DMA = pltpu.SemaphoreType.DMA
MARGIN = 4 << 20
ROOM = 60 * 1024 * 1024


def grant(*shapes):
    return MARGIN + sum(int(np.prod(s)) * np.dtype(d).itemsize for s, d in shapes)


def shards_of(refs, part):
    for ref in refs:
        for i in range(ref.shape[0] // part):
            yield ref.at[i * part : (i + 1) * part, :]


def block(r, side):
    return pl.ds(pl.multiple_of(r * side, side), side)


def forward_kernel(n_in, n_out, part, rows_s, offs_s, *refs):
    x_refs, refs = refs[:n_in], refs[n_in:]
    w_ref, cot, gelu_ref, slopes = refs[:4]
    dx_refs, (xt, xs, acc, gelu, w, out_sem, w_sem) = refs[4 : 4 + n_out], refs[4 + n_out :]
    cols, slots, side, _ = w.shape
    blocks = xs.shape[0]

    def out(c):
        target = gelu_ref.at[:, block(c, side)]
        return pltpu.make_async_copy(gelu.at[c], target, out_sem.at[c])

    def weights(c):
        return pltpu.make_async_copy(w_ref.at[c], w.at[c], w_sem.at[c])

    def load(c, carry):
        weights(c).start()
        return carry

    lax.fori_loop(0, cols, load, 0)
    for j, shard in enumerate(shards_of(x_refs, part)):
        xt[pl.ds(pl.multiple_of(offs_s[j], 16), part), :] = shard[...]

    def turn(r, carry):
        xs[r] = xt[block(r, side), :].T
        acc[block(r, side), :] = jnp.zeros((side, acc.shape[1]), acc.dtype)
        return carry

    lax.fori_loop(0, blocks, turn, 0, unroll=4)
    step = 2 if slots % 2 == 0 else 1

    def activate(c, v):
        v2 = v * v
        t = jnp.tanh(SQRT_2_PI * (v + CUBIC * (v * v2)))
        half = 0.5 * (1.0 + t)
        gelu[c] = (v * half).astype(gelu.dtype)
        slope = half + (0.5 * v) * (1.0 - t * t) * (SQRT_2_PI * (1.0 + (3.0 * CUBIC) * v2))
        slope = cot[:, block(c, side)].astype(jnp.float32) * slope
        slopes[:, block(c, side)] = slope.astype(slopes.dtype)

    def ahead(c, k):
        picked = jnp.concatenate([xs[rows_s[c, k + i]] for i in range(step)], axis=1)
        right = w[c, k : k + step].reshape(step * side, side)
        return jnp.dot(picked, right, preferred_element_type=jnp.float32)

    def back(c, k, turned):
        left = w[c, k : k + step].reshape(step * side, side)
        part_sum = jnp.dot(left, turned, preferred_element_type=jnp.float32)
        for i in range(step):
            acc[block(rows_s[c, k + i], side), :] += part_sum[i * side : (i + 1) * side]

    def one(c, carry):
        out(c).start()
        weights(c + 1).wait()
        turned = slopes[:, block(c, side)].T
        v = 0.0
        for k in range(0, slots, step):
            v = v + ahead(c + 1, k)
            back(c, k, turned)
        activate(c + 1, v)
        return carry

    weights(0).wait()
    activate(0, sum(ahead(0, k) for k in range(0, slots, step)))
    lax.fori_loop(0, cols - 1, one, 0)
    out(cols - 1).start()
    turned = slopes[:, block(cols - 1, side)].T
    for k in range(0, slots, step):
        back(cols - 1, k, turned)

    for j, shard in enumerate(shards_of(dx_refs, part)):
        rows = pl.ds(pl.multiple_of(offs_s[j], 16), part)
        shard[...] = acc[rows, :].astype(shard.dtype)

    def drain(c, carry):
        out(c).wait()
        return carry

    lax.fori_loop(0, cols, drain, 0)


def forward(arrays, part, offs, weights, rows, cot, outs):
    cols, _, side, _ = weights.shape
    tokens = arrays[0].shape[1]
    features = sum(a.shape[0] for a in arrays)
    blocks = features // side
    scratch = [
        ((features, tokens), jnp.bfloat16),
        ((blocks, tokens, side), jnp.bfloat16),
        ((features, tokens), jnp.float32),
        ((cols, tokens, side), jnp.bfloat16),
        (weights.shape, jnp.bfloat16),
    ]
    return pl.pallas_call(
        functools.partial(forward_kernel, len(arrays), len(outs), part),
        grid_spec=pltpu.PrefetchScalarGridSpec(
            num_scalar_prefetch=2,
            in_specs=[VMEM] * len(arrays) + [HBM, VMEM],
            out_specs=[HBM, VMEM] + [VMEM] * len(outs),
            scratch_shapes=[pltpu.VMEM(*s) for s in scratch] + [DMA((cols,))] * 2,
        ),
        out_shape=[jax.ShapeDtypeStruct((tokens, cols * side), jnp.bfloat16)] * 2
        + [jax.ShapeDtypeStruct((m * part, tokens), jnp.bfloat16) for m in outs],
        compiler_params=pltpu.CompilerParams(
            vmem_limit_bytes=max(grant(*scratch), min(ROOM - 2 * weights.size, 48 << 20))
        ),
        cost_estimate=pl.CostEstimate(
            flops=4 * tokens * weights.size,
            bytes_accessed=2 * weights.size,
            transcendentals=tokens * cols * side,
        ),
        name="forward",
    )(rows, offs, *arrays, weights, cot)


def assemble_kernel(n_planes, n_in, part, offs_s, *refs):
    x_refs, xt = refs[:-1], refs[-1]
    tokens = x_refs[0].shape[1]
    for p in range(n_planes):
        for j, shard in enumerate(shards_of(x_refs[p * n_in : (p + 1) * n_in], part)):
            rows = pl.ds(pl.multiple_of(offs_s[j], 16), part)
            xt[rows, p * tokens : (p + 1) * tokens] = shard[...]


def assemble(planes, part, offs):
    arrays = [a for plane in planes for a in plane]
    rows = sum(a.shape[0] for a in planes[0])
    return pl.pallas_call(
        functools.partial(assemble_kernel, len(planes), len(planes[0]), part),
        grid_spec=pltpu.PrefetchScalarGridSpec(
            num_scalar_prefetch=1, in_specs=[VMEM] * len(arrays), out_specs=VMEM
        ),
        out_shape=jax.ShapeDtypeStruct((rows, len(planes) * arrays[0].shape[1]), jnp.bfloat16),
        compiler_params=pltpu.CompilerParams(vmem_limit_bytes=MARGIN),
        name="assemble",
    )(offs, *arrays)


def weight_kernel(n_planes, rows_s, half_s, xt, *refs):
    slope_refs, (out_ref, out, out_sem) = refs[:n_planes], refs[n_planes:]
    cols, slots, side, _ = out.shape

    def result(c):
        return pltpu.make_async_copy(out.at[c], out_ref.at[c], out_sem.at[c])

    def one(c, carry):
        right = jnp.concatenate([ref[:, block(c, side)] for ref in slope_refs], axis=0)
        for k in range(slots):
            left = xt[block(rows_s[c, half_s[0] * slots + k], side), :]
            out[c, k] = jnp.dot(left, right, preferred_element_type=jnp.float32)
        result(c).start()
        return carry

    lax.fori_loop(0, cols, one, 0, unroll=4 if cols % 4 == 0 else 1)

    def drain(c, carry):
        result(c).wait()
        return carry

    lax.fori_loop(0, cols, drain, 0)


def weight_grad(features, slopes, rows, half, slots, side):
    cols = rows.shape[0]
    tokens = slopes[0].shape[0]
    scratch = [((cols, slots, side, side), jnp.float32)]
    return pl.pallas_call(
        functools.partial(weight_kernel, len(slopes)),
        grid_spec=pltpu.PrefetchScalarGridSpec(
            num_scalar_prefetch=2,
            in_specs=[VMEM] * (1 + len(slopes)),
            out_specs=HBM,
            scratch_shapes=[pltpu.VMEM(*s) for s in scratch] + [DMA((cols,))],
        ),
        out_shape=jax.ShapeDtypeStruct((cols, slots, side, side), jnp.float32),
        compiler_params=pltpu.CompilerParams(vmem_limit_bytes=grant(*scratch)),
        cost_estimate=pl.CostEstimate(
            flops=2 * len(slopes) * tokens * cols * slots * side * side,
            bytes_accessed=4 * cols * slots * side * side,
            transcendentals=0,
        ),
        name="weight_grad",
    )(rows, half, features, *slopes)


def pack_kernel(*refs):
    out, start = refs[-1], 0
    for ref in refs[:-1]:
        out[start : start + ref.shape[0], :] = ref[...]
        start += ref.shape[0]


def pack(arrays):
    rows = sum(a.shape[0] for a in arrays)
    return pl.pallas_call(
        pack_kernel,
        in_specs=[VMEM] * len(arrays),
        out_specs=VMEM,
        out_shape=jax.ShapeDtypeStruct((rows, arrays[0].shape[1]), arrays[0].dtype),
        compiler_params=pltpu.CompilerParams(vmem_limit_bytes=MARGIN),
        name="pack",
    )(*arrays)


def stage_kernel(*refs):
    half = len(refs) // 2
    for source, target in zip(refs[:half], refs[half:]):
        target[...] = source[...]


def stage(*arrays):
    return pl.pallas_call(
        stage_kernel,
        in_specs=[VMEM] * len(arrays),
        out_specs=[VMEM] * len(arrays),
        out_shape=[jax.ShapeDtypeStruct(a.shape, a.dtype) for a in arrays],
        compiler_params=pltpu.CompilerParams(vmem_limit_bytes=MARGIN),
        name="stage",
    )(*arrays)


def sum_kernel(plan, part, n_in, *refs):
    ins, outs = refs[:n_in], refs[n_in:]
    for terms, out in zip(plan, outs):
        total = 0.0
        for a, i in terms:
            total = total + ins[a][i * part : (i + 1) * part, :].astype(jnp.float32)
        out[...] = total.astype(out.dtype)


def add_parts(arrays, plan, part):
    tokens = arrays[0].shape[1]
    return pl.pallas_call(
        functools.partial(sum_kernel, plan, part, len(arrays)),
        in_specs=[VMEM] * len(arrays),
        out_specs=[VMEM] * len(plan),
        out_shape=[jax.ShapeDtypeStruct((part, tokens), jnp.bfloat16)] * len(plan),
        compiler_params=pltpu.CompilerParams(vmem_limit_bytes=MARGIN),
        name="add_parts",
    )(*arrays)


def direct(n, mp):
    return n % (CORES * SIDES) == 0 and 2 <= n // (CORES * SIDES) <= MAX_LINE and mp == 2


def body(activations, block_values, block_rows, cotangent):
    n, mp = lax.axis_size("dp"), lax.axis_size("mp")
    me, half = lax.axis_index("dp"), lax.axis_index("mp")
    side, slot_count = block_values.shape[2], block_values.shape[1]
    own = activations.T
    part, _ = own.shape
    half = half.astype(jnp.int32).reshape(1)
    chip = CORES * SIDES
    line = n // chip
    if not direct(n, mp):
        offs = jnp.zeros((1,), jnp.int32)
        x_own = lax.all_gather(own, "dp", axis=0, tiled=True)
        x_all = lax.all_gather(x_own, "mp", axis=0)
        whole = x_own.shape[0]
        gelu_out, slopes, dx = forward(
            [x_own], whole, offs, block_values, block_rows, cotangent, [1]
        )
        slopes_all = lax.all_gather(slopes, "mp", axis=0)
        block_grad = weight_grad(
            assemble([[x_all[p]] for p in range(mp)], whole, offs),
            [slopes_all[p] for p in range(mp)],
            block_rows,
            half,
            slot_count // mp,
            side,
        )
        dx = dx.astype(jnp.float32)
        dx = lax.psum_scatter(dx, "dp", scatter_dimension=0, tiled=True)
        return gelu_out, dx.astype(jnp.bfloat16).T, block_grad

    def along(z, k):
        return z ^ k if line & (line - 1) == 0 else (z + k) % line

    def permute(a, k, s, q):
        def source(i):
            z, x, core = i // chip, i // CORES % SIDES, i % CORES
            return (along(z, k) * SIDES + (x ^ s)) * CORES + (core ^ q)

        return lax.ppermute(a, "dp", [(source(i), i) for i in range(n)])

    def back_to(k):
        return next(i for i in range(line) if along(along(0, k), i) == 0)

    def across(a):
        return lax.ppermute(a, "mp", [(i, i ^ 1) for i in range(mp)])

    rel = [(k, s, q) for q in range(CORES) for s in range(SIDES) for k in range(line)]
    ks, ss, qs = (np.array(v, np.int32) for v in zip(*rel))
    z, x, core = me // chip, me // CORES % SIDES, me % CORES
    offs = ((along(z, ks) * SIDES + (x ^ ss)) * CORES + (core ^ qs)) * part
    offs = offs.astype(jnp.int32)

    cotangent, block_rows = stage(cotangent, block_rows)
    near = [permute(own, k, 0, 0) if k else own for k in range(line)]
    side_x = [permute(a, 0, 1, 0) for a in near]
    x_own, x_far = [], []
    for s, arrays in enumerate((near, side_x)):
        x_own.append(pack(arrays))
        x_far.append(across(x_own[s]))
    for s in range(SIDES):
        x_own.append(permute(x_own[s], 0, 0, 1))
        x_far.append(permute(x_far[s], 0, 0, 1))

    gelu_out, slopes, keep0, keep1, give0, give1 = forward(
        x_own, part, offs, block_values, block_rows, cotangent, [line] * 4
    )
    got1 = permute(give1, 0, 0, 1)
    got0 = permute(give0, 0, 0, 1)
    slopes_far = across(slopes)
    first = add_parts([keep1, got1], [[(0, k), (1, k)] for k in range(1, line)], part)
    chips = add_parts([keep1, got1], [[(0, 0), (1, 0)]], part) + first
    pairs = [permute(a, 0, 1, 0) for a in chips]
    total = (
        keep0[:part].astype(jnp.float32)
        + got0[:part].astype(jnp.float32)
        + pairs[0].astype(jnp.float32)
    )
    for k in range(1, line):
        (mine,) = add_parts([keep0, got0, pairs[k]], [[(0, k), (1, k), (2, 0)]], part)
        total = total + permute(mine, back_to(k), 0, 0).astype(jnp.float32)
    features = assemble([x_own, x_far], part, offs)
    block_grad = weight_grad(
        features,
        [slopes, slopes_far],
        block_rows,
        half,
        slot_count // mp,
        side,
    )
    return gelu_out, total.astype(jnp.bfloat16).T, block_grad


def solution(mesh):
    in_specs = (P("mp", "dp"), P("dp", None, None, None), P("dp", None), P("mp", "dp"))
    out_specs = (P("mp", "dp"), P("mp", "dp"), P("dp", "mp", None, None))
    step = jax.shard_map(body, mesh=mesh, in_specs=in_specs, out_specs=out_specs, check_vma=False)
    n, mp = mesh.shape["dp"], mesh.shape["mp"]
    if not direct(n, mp):
        return step
    return step
```
